32 devices in a mesh: dp: 4 (over y, core), expert: 2 (over x), group: 4 (over z).
Axes of the slice: x: 2, y: 2, z: 4, core: 2. Of those that a mesh axis runs over, the one named last changes fastest.
Arguments:
- tokens: bfloat16 [256, 7168], P(('dp', 'group')), may hold values from -6 to 6
- expert_ids: int32 [256, 8], P(('dp', 'group')), may hold values from 0 to 255, all different within a row; in each aligned block of 16 rows (0 to 15, 16 to 31, ...) at most 2 rows name the same one
- gate_values: bfloat16 [256, 8], P(('dp', 'group')), may hold values from 0.099609375 to 1
- gate_up: bfloat16 [2, 7168, 2, 2048], P('expert', None, None, 'group'), may hold values from -0.0625 to 0.0625
- down_weight: bfloat16 [2, 2048, 7168], P('expert', 'group'), may hold values from -0.125 to 0.125
- shared_gate_up: bfloat16 [7168, 2, 2048], P('expert', None, 'group'), may hold values from -0.0625 to 0.0625
- shared_down: bfloat16 [2048, 7168], P('group', 'expert'), may hold values from -0.125 to 0.125
Outputs:
- mixed: bfloat16 [256, 7168], P(('dp', 'group'), 'expert')
The draws below stay inside these ranges and needn't reach their ends.
Inputs may be any that keep to these rules, and one draw needn't show every extreme that they name: `expert_ids`: each row names 8 different routed experts. In each aligned block of 16 rows (the rows of one device) no expert is named by more than 2 rows, and in some blocks one is named by exactly 2 rows.
All inputs are finite; a program needn't handle non-finite values.
Results may differ from the reference program's by a relative error of at most 0.028.
Values may be sent and summed in bfloat16 or wider, within the bound.
No kernel may reach another device: no remote copies, remote signals or barrier semaphores. Data moves between devices by JAX's collectives and lax.ppermute only.
A program may use at most 128 MiB of HBM per device.

```python
import math
import jax
import jax.numpy as jnp
import numpy as np

D = 7168
FF = 2048
ROUTED = 256
TOPK = 8
TOK_DEV = 16
CAP = 2
SLOTS = 2
FF_DEV = 512
TOKENS = 256
N_GROUP = 4


def block_levels(rng, dims, pieces, smallest, top_value):
    gain, own = 1.0, jax.random.fold_in(rng, 6)
    for position, parts in pieces:
        heights = jnp.exp(jax.random.uniform(jax.random.fold_in(own, position), (parts,), jnp.float32, smallest / len(pieces), top_value / len(pieces)))
        gain = gain * jnp.repeat(heights, dims[position] // parts).reshape([-1 if axis == position else 1 for axis in range(len(dims))])
    return gain


def routed_block(stream_key, own, number, rows, number_of, top, limit, skew):
    ranking = jax.random.permutation(stream_key, number_of)
    crowded, common = portions_of(number_of, rows * top, limit, skew, True), portions_of(number_of, rows * top, limit, skew, False)
    places = jnp.arange(number_of)

    def named(tallies, rotation):
        used = int((tallies > 0).sum())
        fixed = max(1, used // 4)
        moved = fixed + (places - fixed + rotation * (used - fixed)) % max(1, number_of - fixed)
        return jnp.zeros((number_of,), jnp.int32).at[ranking[jnp.where(places < fixed, places, moved)]].set(jnp.asarray(tallies, jnp.int32))

    tallies = jnp.where(number % 4 == 0, named(crowded, number // 4), named(common, number - number // 4 - 1))
    mixed = jax.random.permutation(jax.random.fold_in(own, 3), number_of)
    source_of, sink = mixed[0:number_of // 2 * 2:2], mixed[1:number_of // 2 * 2:2]
    room = jnp.minimum(tallies[source_of] - 1, limit - tallies[sink]) // 2
    room = jnp.where((source_of == ranking[0]) | (sink == ranking[0]) | (tallies[sink] == 0), 0, jnp.maximum(room, 0))
    moved = jax.random.randint(jax.random.fold_in(own, 4), (number_of // 2,), 0, 1 << 20) % (room + 1)
    tallies = tallies.at[source_of].add(-moved).at[sink].add(moved)
    members = jnp.searchsorted(jnp.cumsum(tallies), jnp.arange(rows * top), side="right").astype(jnp.int32)
    table = members.reshape(top, rows).T
    table = table[jax.random.permutation(jax.random.fold_in(own, 1), rows)]
    rotation = jax.random.randint(jax.random.fold_in(own, 2), (rows, 1), 0, top)
    return jnp.take_along_axis(table, (jnp.arange(top)[None, :] + rotation) % top, axis=1)


def portions_of(amount, total, reach, lean, full):
    weights = [(1 << 20) // math.isqrt(rank ** lean) + 1 for rank in range(1, amount + 1)]
    largest = reach if full else min(reach, max(-(-total // amount), total * weights[0] // sum(weights)))
    least = 1 if total - largest >= amount - 1 else 0
    counts, rest = [largest] + [least] * (amount - 1), total - largest - least * (amount - 1)
    while rest > 0:
        movable = [i for i in range(1, amount) if counts[i] < largest] or [i for i in range(1, amount) if counts[i] < reach]
        pool, left = sum([weights[i] for i in movable]), rest
        for i in movable:
            more = min(reach - counts[i], max(1, left * weights[i] // pool), rest)
            counts[i] = counts[i] + more
            rest = rest - more
    return np.array(counts)


def centred(key, extent, width, bound, pieces=(), dtype=jnp.bfloat16):
    result = jax.random.normal(key, extent, jnp.float32) * width
    if len(pieces) > 0:
        result = block_levels(key, extent, pieces, -0.22, 0.18) * result
    return jnp.clip(result, min=-bound, max=bound).astype(dtype)


def setup_inputs(seed: int = 0) -> dict:
    streams_of = jax.random.split(jax.random.key(seed), 8)
    tokens = centred(streams_of[0], (TOKENS, D), 1.0, 6.0, ((0, 16),))
    expert_ids_keys = jax.random.split(jax.random.fold_in(streams_of[1], 1), TOKENS // TOK_DEV)
    expert_ids_turns = jax.random.permutation(jax.random.fold_in(streams_of[1], 3), TOKENS // TOK_DEV)
    expert_ids = jax.vmap(lambda own, number: routed_block(jax.random.fold_in(streams_of[1], 2), own, number, TOK_DEV, ROUTED, TOPK, CAP, 2))(expert_ids_keys, expert_ids_turns).reshape((TOKENS, TOPK))
    gate_values = jnp.clip(jnp.exp(math.log(1.0) - 2.306499 * jax.random.uniform(streams_of[2], (TOKENS, TOPK), jnp.float32) ** block_levels(streams_of[2], (TOKENS, TOPK), ((0, 16),), -0.2, 0.2)), 0.099609375, 1.0).astype(jnp.bfloat16)
    gate_up = centred(streams_of[3], (SLOTS, D, 2, FF), D ** -0.5, 0.0625, ((0, 2), (3, 4)))
    down_weight = centred(streams_of[4], (SLOTS, FF, D), FF ** -0.5, 0.125, ((0, 2), (1, 4)))
    shared_gate_up = centred(streams_of[5], (D, 2, FF), D ** -0.5, 0.0625, ((0, 2), (2, 4)))
    shared_down = centred(streams_of[6], (FF, D), FF ** -0.5, 0.125, ((0, 4), (1, 2)))
    return {"tokens": tokens, "expert_ids": expert_ids, "gate_values": gate_values, "gate_up": gate_up, "down_weight": down_weight, "shared_gate_up": shared_gate_up, "shared_down": shared_down}


def reference(tokens, expert_ids, gate_values, gate_up, down_weight, shared_gate_up, shared_down):
    accumulated = jnp.zeros((TOKENS, D), jnp.float32)
    for slot_index in range(SLOTS):
        chosen = expert_ids == slot_index
        slot_weight = jnp.sum(jnp.where(chosen, gate_values.astype(jnp.float32), jnp.float32(0.0)), axis=1)
        gate_part = jnp.dot(tokens, gate_up[slot_index, :, 0, :], preferred_element_type=jnp.float32)
        up_part = jnp.dot(tokens, gate_up[slot_index, :, 1, :], preferred_element_type=jnp.float32)
        hidden = (jax.nn.silu(gate_part) * up_part).astype(jnp.bfloat16)
        for block_index in range(N_GROUP):
            first_unit = block_index * FF_DEV
            product = jnp.dot(hidden[:, first_unit:first_unit + FF_DEV],
                              down_weight[slot_index, first_unit:first_unit + FF_DEV, :],
                              preferred_element_type=jnp.float32)
            slot_term = (product * slot_weight[:, None]).astype(jnp.bfloat16)
            accumulated = accumulated + slot_term.astype(jnp.float32)
    shared_gate = jnp.dot(tokens, shared_gate_up[:, 0, :], preferred_element_type=jnp.float32)
    shared_up = jnp.dot(tokens, shared_gate_up[:, 1, :], preferred_element_type=jnp.float32)
    shared_hidden = (jax.nn.silu(shared_gate) * shared_up).astype(jnp.bfloat16)
    for block_index in range(N_GROUP):
        first_unit = block_index * FF_DEV
        shared_term = jnp.dot(shared_hidden[:, first_unit:first_unit + FF_DEV],
                              shared_down[first_unit:first_unit + FF_DEV, :],
                              preferred_element_type=jnp.float32).astype(jnp.bfloat16)
        accumulated = accumulated + shared_term.astype(jnp.float32)
    return accumulated.astype(jnp.bfloat16)
```

```python
import jax
import jax.numpy as jnp
from jax import lax
from jax.sharding import PartitionSpec as P

CAP = 2
FORM = "einsum"
GATHER = "permute"
SCATTER = "permute"


def gated(rows, weight):
    model_width, _, units = weight.shape
    if FORM == "interleave":
        zero = jnp.zeros_like(rows)
        lhs = jnp.stack([jnp.stack([rows, zero], 2), jnp.stack([zero, rows], 2)])
        lhs = lhs.reshape(2 * rows.shape[0], 2 * model_width)
        out = jnp.dot(lhs, weight.reshape(2 * model_width, units), preferred_element_type=jnp.float32)
        return out[: rows.shape[0]], out[rows.shape[0]:]
    if FORM == "slice":
        return tuple(jnp.dot(rows, weight[:, i], preferred_element_type=jnp.float32) for i in (0, 1))
    if FORM == "einsum":
        out = jnp.einsum("td,dgf->gtf", rows, weight, preferred_element_type=jnp.float32)
        return out[0], out[1]
    out = jnp.dot(rows, weight.reshape(model_width, 2 * units), preferred_element_type=jnp.float32)
    return out[:, :units], out[:, units:]


def swiglu(gate, up):
    return (jax.nn.silu(gate) * up).astype(jnp.bfloat16)


def gather_blocks(block, axis):
    size = lax.axis_size(axis)
    if GATHER == "ag":
        return lax.all_gather(block, axis)
    if GATHER == "a2a":
        return lax.all_to_all(jnp.broadcast_to(block[None], (size,) + block.shape), axis, 0, 0)
    pieces = [block]
    for step in range(1, size):
        pieces.append(lax.ppermute(block, axis, [(i, (i - step) % size) for i in range(size)]))
    return jnp.stack(pieces)


def exchange(blocks, axis):
    size = lax.axis_size(axis)
    arrived = [blocks[0]]
    for step in range(1, size):
        arrived.append(lax.ppermute(blocks[step], axis, [(i, (i + step) % size) for i in range(size)]))
    return arrived


def per_device(tokens, expert_ids, gate_values, gate_up, down_weight, shared_gate_up, shared_down):
    experts, groups = lax.axis_size("expert"), lax.axis_size("group")
    me = lax.axis_index("expert")
    count, width = tokens.shape
    columns = shared_gate_up.shape[0]
    units = shared_gate_up.shape[2]

    slots = jnp.arange(experts, dtype=jnp.int32)
    named = expert_ids[None] == slots[:, None, None]
    chosen = jnp.any(named, axis=2)
    weight = jnp.sum(jnp.where(named, gate_values.astype(jnp.float32)[None], 0.0), axis=2)
    rank = jnp.sum(
        jnp.where(jnp.tril(jnp.ones((count, count), jnp.bool_), -1)[None], chosen[:, None, :], False).astype(jnp.int32),
        axis=2,
    )
    places = jnp.arange(CAP, dtype=jnp.int32)[None, :, None]
    selection = (chosen[:, None, :] & (rank[:, None, :] == places))
    mine = lax.dynamic_index_in_dim(selection, me, 0, keepdims=False).astype(jnp.bfloat16)
    rows = jnp.dot(mine, tokens, preferred_element_type=jnp.float32).astype(jnp.bfloat16)

    own_columns = lax.dynamic_slice_in_dim(tokens, me * columns, columns, 1)
    all_rows = gather_blocks(rows, "group").reshape(groups * CAP, width)
    all_columns = gather_blocks(own_columns, "group").reshape(groups * count, columns)

    shared_gate, shared_up = gated(all_columns, shared_gate_up)
    partial = jnp.concatenate([shared_gate, shared_up], 1)
    if experts == 2:
        other = lax.ppermute(partial.astype(jnp.bfloat16), "expert", [(0, 1), (1, 0)])
        pre = partial + other.astype(jnp.float32)
    else:
        pre = lax.psum(partial.astype(jnp.bfloat16), "expert").astype(jnp.float32)

    hidden = swiglu(*gated(all_rows, gate_up[0]))
    product = jnp.dot(hidden, down_weight[0], preferred_element_type=jnp.float32).astype(jnp.bfloat16)
    product = product.reshape(groups * CAP, experts, columns)
    if experts == 2:
        keep = lax.dynamic_index_in_dim(product, me, 1, keepdims=False)
        away = lax.dynamic_index_in_dim(product, 1 - me, 1, keepdims=False)
        came = lax.ppermute(away, "expert", [(0, 1), (1, 0)])
        first = jnp.where(me == 0, keep, came)
        second = jnp.where(me == 0, came, keep)
        routed = jnp.stack([first, second]).reshape(experts, groups, CAP, columns)
    else:
        routed = lax.all_to_all(product, "expert", 1, 0).reshape(experts, groups, CAP, columns)

    shared_hidden = swiglu(pre[:, :units], pre[:, units:])
    shared = jnp.dot(shared_hidden, shared_down, preferred_element_type=jnp.float32).astype(jnp.bfloat16)

    arrived = exchange(shared.reshape(groups, count, columns), "group")
    routed_arrived = exchange(jnp.swapaxes(routed, 0, 1).reshape(groups, experts * CAP, columns), "group")
    total = sum(a.astype(jnp.float32) for a in arrived)
    terms = sum(a.astype(jnp.float32) for a in routed_arrived)
    spread = jnp.where(selection, weight[:, None, :], 0.0).reshape(experts * CAP, count)
    for j in range(experts * CAP):
        total = total + spread[j][:, None] * terms[j][None, :]
    return total.astype(jnp.bfloat16)


def solution(mesh):
    in_specs = (
        P(("dp", "group"), None),
        P(("dp", "group"), None),
        P(("dp", "group"), None),
        P("expert", None, None, "group"),
        P("expert", "group", None),
        P("expert", None, "group"),
        P("group", "expert"),
    )
    out_specs = P(("dp", "group"), "expert")
    return jax.shard_map(
        per_device, mesh=mesh, in_specs=in_specs, out_specs=out_specs, check_vma=False
    )
```

```python
import jax
import jax.numpy as jnp
from jax import lax
from jax.sharding import PartitionSpec as P


CAP = 2


def gated(rows, weight):
    out = jnp.einsum("td,dgf->gtf", rows, weight, preferred_element_type=jnp.float32)
    return out[0], out[1]


def swiglu(gate, up):
    return (jax.nn.silu(gate) * up).astype(jnp.bfloat16)


def gather_blocks(block, axis):
    size = lax.axis_size(axis)
    pieces = [block]
    for step in range(1, size):
        pieces.append(lax.ppermute(block, axis, [(i, (i - step) % size) for i in range(size)]))
    return jnp.concatenate(pieces, 0)


def exchange(blocks, axis):
    size = lax.axis_size(axis)
    arrived = [blocks[0]]
    for step in range(1, size):
        arrived.append(lax.ppermute(blocks[step], axis, [(i, (i + step) % size) for i in range(size)]))
    return arrived


def per_device(tokens, expert_ids, gate_values, gate_up, down_weight, shared_gate_up, shared_down):
    experts, groups = lax.axis_size("expert"), lax.axis_size("group")
    me = lax.axis_index("expert")
    count, _ = tokens.shape
    columns = shared_gate_up.shape[0]
    units = shared_gate_up.shape[2]

    slots = jnp.arange(experts, dtype=jnp.int32)
    named = expert_ids[None] == slots[:, None, None]
    chosen = jnp.any(named, axis=2)
    weight = jnp.sum(jnp.where(named, gate_values.astype(jnp.float32)[None], 0.0), axis=2)
    rank = jnp.sum(
        jnp.where(jnp.tril(jnp.ones((count, count), jnp.bool_), -1)[None], chosen[:, None, :], False).astype(jnp.int32),
        axis=2,
    )
    places = jnp.arange(CAP, dtype=jnp.int32)[None, :, None]
    selection = (chosen[:, None, :] & (rank[:, None, :] == places))
    mine = lax.dynamic_index_in_dim(selection, me, 0, keepdims=False).astype(jnp.bfloat16)
    rows = jnp.dot(mine, tokens, preferred_element_type=jnp.float32).astype(jnp.bfloat16)

    own_columns = lax.dynamic_slice_in_dim(tokens, me * columns, columns, 1)
    all_rows = gather_blocks(rows, "group")
    all_columns = gather_blocks(own_columns, "group")

    shared_gate, shared_up = gated(all_columns, shared_gate_up)
    partial = jnp.concatenate([shared_gate, shared_up], 1)
    if experts == 2:
        other = lax.ppermute(partial.astype(jnp.bfloat16), "expert", [(0, 1), (1, 0)])
        pre = partial + other.astype(jnp.float32)
    else:
        pre = lax.psum(partial.astype(jnp.bfloat16), "expert").astype(jnp.float32)

    hidden = swiglu(*gated(all_rows, gate_up[0]))
    product = jnp.dot(hidden, down_weight[0], preferred_element_type=jnp.float32).astype(jnp.bfloat16)
    product = product.reshape(groups * CAP, experts, columns)
    if experts == 2:
        keep = lax.dynamic_index_in_dim(product, me, 1, keepdims=False)
        away = lax.dynamic_index_in_dim(product, 1 - me, 1, keepdims=False)
        came = lax.ppermute(away, "expert", [(0, 1), (1, 0)])
        first = jnp.where(me == 0, keep, came)
        second = jnp.where(me == 0, came, keep)
        routed = jnp.stack([first, second]).reshape(experts, groups, CAP, columns)
    else:
        routed = lax.all_to_all(product, "expert", 1, 0).reshape(experts, groups, CAP, columns)

    shared_hidden = swiglu(pre[:, :units], pre[:, units:])
    shared = jnp.dot(shared_hidden, shared_down, preferred_element_type=jnp.float32).astype(jnp.bfloat16)

    arrived = exchange(shared.reshape(groups, count, columns), "group")
    routed_blocks = jnp.swapaxes(routed, 0, 1).reshape(groups, experts * CAP, columns)
    routed_arrived = exchange(routed_blocks, "group")
    total = sum(a.astype(jnp.float32) for a in arrived)
    terms = sum(a.astype(jnp.float32) for a in routed_arrived)
    spread = jnp.where(selection, weight[:, None, :], 0.0).reshape(experts * CAP, count)
    for j in range(experts * CAP):
        total = total + spread[j][:, None] * terms[j][None, :]
    return total.astype(jnp.bfloat16)


def solution(mesh):
    in_specs = (
        P(("dp", "group"), None),
        P(("dp", "group"), None),
        P(("dp", "group"), None),
        P("expert", None, None, "group"),
        P("expert", "group", None),
        P("expert", None, "group"),
        P("group", "expert"),
    )
    out_specs = P(("dp", "group"), "expert")

    return jax.shard_map(per_device, mesh=mesh, in_specs=in_specs, out_specs=out_specs, check_vma=False)
```

```python
import jax
import jax.numpy as jnp
from jax import lax
from jax.sharding import PartitionSpec as P


CAP = 2


def gated(rows, weight):
    out = jnp.einsum("td,dgf->gtf", rows, weight, preferred_element_type=jnp.float32)
    return out[0], out[1]


def swiglu(gate, up):
    return (jax.nn.silu(gate) * up).astype(jnp.bfloat16)


def gather_blocks(block, axis):
    size = lax.axis_size(axis)
    pieces = [block]
    for step in range(1, size):
        pieces.append(lax.ppermute(block, axis, [(i, (i - step) % size) for i in range(size)]))
    return pieces


def exchange(blocks, axis):
    size = lax.axis_size(axis)
    arrived = [blocks[0]]
    for step in range(1, size):
        arrived.append(lax.ppermute(blocks[step], axis, [(i, (i + step) % size) for i in range(size)]))
    return arrived


def per_device(tokens, expert_ids, gate_values, gate_up, down_weight, shared_gate_up, shared_down):
    experts, groups = lax.axis_size("expert"), lax.axis_size("group")
    me = lax.axis_index("expert")
    count, width = tokens.shape
    columns = shared_gate_up.shape[0]
    units = shared_gate_up.shape[2]

    slots = jnp.arange(experts, dtype=jnp.int32)
    named = expert_ids[None] == slots[:, None, None]
    chosen = jnp.any(named, axis=2)
    weight = jnp.sum(jnp.where(named, gate_values.astype(jnp.float32)[None], 0.0), axis=2)
    rank = jnp.sum(
        jnp.where(jnp.tril(jnp.ones((count, count), jnp.bool_), -1)[None], chosen[:, None, :], False).astype(jnp.int32),
        axis=2,
    )
    places = jnp.arange(CAP, dtype=jnp.int32)[None, :, None]
    selection = (chosen[:, None, :] & (rank[:, None, :] == places))
    mine = lax.dynamic_index_in_dim(selection, me, 0, keepdims=False).astype(jnp.bfloat16)
    rows = jnp.dot(mine, tokens, preferred_element_type=jnp.float32).astype(jnp.bfloat16)

    own_columns = lax.dynamic_slice_in_dim(tokens, me * columns, columns, 1)
    all_rows = jnp.stack(gather_blocks(rows, "group")).reshape(groups * CAP, width)
    all_columns = jnp.concatenate(gather_blocks(own_columns, "group"), 0)

    shared_gate, shared_up = gated(all_columns, shared_gate_up)
    partial = jnp.concatenate([shared_gate, shared_up], 1)
    if experts == 2:
        other = lax.ppermute(partial.astype(jnp.bfloat16), "expert", [(0, 1), (1, 0)])
        pre = partial + other.astype(jnp.float32)
    else:
        pre = lax.psum(partial.astype(jnp.bfloat16), "expert").astype(jnp.float32)

    hidden = swiglu(*gated(all_rows, gate_up[0]))
    product = jnp.dot(hidden, down_weight[0], preferred_element_type=jnp.float32).astype(jnp.bfloat16)
    product = product.reshape(groups * CAP, experts, columns)
    if experts == 2:
        keep = lax.dynamic_index_in_dim(product, me, 1, keepdims=False)
        away = lax.dynamic_index_in_dim(product, 1 - me, 1, keepdims=False)
        came = lax.ppermute(away, "expert", [(0, 1), (1, 0)])
        first = jnp.where(me == 0, keep, came)
        second = jnp.where(me == 0, came, keep)
        routed = jnp.stack([first, second]).reshape(experts, groups, CAP, columns)
    else:
        routed = lax.all_to_all(product, "expert", 1, 0).reshape(experts, groups, CAP, columns)

    shared_hidden = swiglu(pre[:, :units], pre[:, units:])
    shared = jnp.dot(shared_hidden, shared_down, preferred_element_type=jnp.float32).astype(jnp.bfloat16)

    arrived = exchange(shared.reshape(groups, count, columns), "group")
    routed_blocks = jnp.swapaxes(routed, 0, 1).reshape(groups, experts * CAP, columns)
    routed_arrived = exchange(routed_blocks, "group")
    total = sum(a.astype(jnp.float32) for a in arrived)
    terms = sum(a.astype(jnp.float32) for a in routed_arrived)
    spread = jnp.where(selection, weight[:, None, :], 0.0).reshape(experts * CAP, count)
    for j in range(experts * CAP):
        total = total + spread[j][:, None] * terms[j][None, :]
    return total.astype(jnp.bfloat16)


def solution(mesh):
    in_specs = (
        P(("dp", "group"), None),
        P(("dp", "group"), None),
        P(("dp", "group"), None),
        P("expert", None, None, "group"),
        P("expert", "group", None),
        P("expert", None, "group"),
        P("group", "expert"),
    )
    out_specs = P(("dp", "group"), "expert")

    return jax.shard_map(per_device, mesh=mesh, in_specs=in_specs, out_specs=out_specs, check_vma=False)
```
